32 devices in a mesh: grp: 8 (over z, y), dir: 4 (over x, core).
Axes of the slice: x: 2, y: 2, z: 4, core: 2. Of those that a mesh axis runs over, the one named last changes fastest.
Arguments:
- currents: bfloat16 [2048, 128], P('grp'), may hold values from -6 to 6
- basis_group: int32 [2048], P('grp'), may hold values from 0 to 1
- projection: bfloat16 [2048, 1024], P('grp', 'dir'), may hold values from -0.5 to 0.5
- filters: bfloat16 [4, 64, 1024], P(None, None, 'dir'), may hold values from -0.25 to 0.25
- pair_src: int32 [128], P('grp'), may hold values from 0 to 7, as said below
- pair_dst: int32 [128], P('grp'), may hold values from 0 to 7, as said below
- pair_type: int32 [128], P('grp'), may hold values from 0 to 3
- live_count: int32 [8], P('grp'), may hold values from 8 to 16, as said below
- send_group: int32 [8, 8], replicated, may hold values from 0 to 1, as said below
- recv_group: int32 [8, 8], replicated, may hold values from 0 to 1, as said below
Outputs:
- field: bfloat16 [2048, 128], P('grp')
The draws below stay inside these ranges and needn't reach their ends.
Inputs may be any that keep to these rules, and one draw needn't show every extreme that they name: `pair_src`: for each reader, its first 8 slots name every owner once. `pair_dst`: for each reader, its first 8 slots name every owner once. `live_count`: some reader has all 16 slots live. `send_group`: each row names every one of the owner's groups at least once. `recv_group`: each row names every one of the owner's groups at least once.
All inputs are finite; a program needn't handle non-finite values.
Results may differ from the reference program's by a relative error of at most 0.0058.
Values may be sent and summed in bfloat16 or wider, within the bound.
No kernel may reach another device: no remote copies, remote signals or barrier semaphores. Data moves between devices by JAX's collectives and lax.ppermute only.
A program may use at most 192 MiB of HBM per device.

```python
import jax
import jax.numpy as jnp
from jax import lax

K = 1024
TAPS = 64
BPG = 128
G_DEV = 2
TYPES = 4
READERS = 8
FAR_DEV = 16
NT = 128
GROUPS = 16
BASIS = 2048


def pair_rows(key, salt):
    keys = jax.random.split(jax.random.fold_in(key, salt), READERS)

    def single_row(row_key):
        first_key, second_key = jax.random.split(row_key)
        head = jax.random.permutation(first_key, READERS).astype(jnp.int32)
        tail = jax.random.randint(second_key, (FAR_DEV - READERS,), 0, READERS).astype(jnp.int32)
        return jnp.concatenate([head, tail])
    return jax.vmap(single_row)(keys).reshape(-1)


def owner_table(key, salt):
    keys = jax.random.split(jax.random.fold_in(key, salt), READERS)

    def single_owner(owner_key):
        first_key, second_key = jax.random.split(owner_key)
        base = jax.random.randint(first_key, (READERS,), 0, G_DEV).astype(jnp.int32)
        places = jax.random.permutation(second_key, READERS)[:G_DEV]
        return base.at[places].set(jnp.arange(G_DEV, dtype=jnp.int32))
    return jax.vmap(single_owner)(keys)


def draw_pair_src(key, part):
    return pair_rows(key, 11)


def draw_pair_dst(key, part):
    return pair_rows(key, 23)


def draw_live_count(key, part):
    first_key, second_key, third_key, fourth_key = jax.random.split(jax.random.fold_in(key, 31), 4)
    span = FAR_DEV - READERS + 1
    extra = jax.random.randint(first_key, (READERS,), 0, span)
    extra = jnp.minimum(extra, jax.random.randint(second_key, (READERS,), 0, span))
    extra = jnp.minimum(extra, jax.random.randint(third_key, (READERS,), 0, span))
    counts = (READERS + extra).astype(jnp.int32)
    heaviest_group = jax.random.randint(fourth_key, (), 0, READERS)
    return counts.at[heaviest_group].set(FAR_DEV)


def draw_send_group(key, part):
    return owner_table(key, 37)


def draw_recv_group(key, part):
    return owner_table(key, 41)


def plant(values, stream_key, least, largest):
    spot = [jax.random.randint(jax.random.fold_in(stream_key, axis), (), 0, length) for axis, length in enumerate(values.shape)]
    widest = values.shape.index(max(values.shape))
    next_to = spot[:widest] + [(spot[widest] + 1) % values.shape[widest]] + spot[widest + 1:]
    return values.at[tuple(spot)].set(least).at[tuple(next_to)].set(largest)


def steps_of(own_key, dims, cuts, least, high):
    factor_of = 1.0
    for position, parts in cuts:
        steps = jax.random.uniform(jax.random.fold_in(jax.random.fold_in(own_key, 6), position), (parts,), jnp.float32, least / len(cuts), high / len(cuts))
        factor_of = factor_of * jnp.repeat(jnp.exp(steps), dims[position] // parts).reshape((-1,) + (1,) * (len(dims) - 1 - position))
    return factor_of


def bell_draw(key, shape, deviation, reach, shards=(), kind=jnp.bfloat16):
    drawn = deviation * jax.random.normal(key, shape, jnp.float32)
    if shards:
        drawn = drawn * steps_of(key, shape, shards, -0.22, 0.18)
    return jnp.clip(drawn, -reach, reach).astype(kind)


def setup_inputs(seed: int = 0) -> dict:
    key_of = jax.random.split(jax.random.key(seed), 11)
    return {
        "currents": bell_draw(key_of[0], (BASIS, NT), 1.0, 6.0, ((0, 8),)),
        "basis_group": plant(jax.random.randint(key_of[1], (BASIS,), 0, G_DEV), jax.random.fold_in(key_of[1], 1), 0, G_DEV - 1).astype(jnp.int32),
        "projection": bell_draw(key_of[2], (BASIS, K), BPG ** -0.5, 0.5, ((0, 8), (1, 4))),
        "filters": bell_draw(key_of[3], (TYPES, TAPS, K), (TAPS * FAR_DEV // G_DEV) ** -0.5, 0.25, ((2, 4),)),
        "pair_src": draw_pair_src(jax.random.fold_in(key_of[10], 71), 0),
        "pair_dst": draw_pair_dst(jax.random.fold_in(key_of[10], 71), 0),
        "pair_type": plant(jax.random.randint(key_of[6], (READERS * FAR_DEV,), 0, TYPES), jax.random.fold_in(key_of[6], 1), 0, TYPES - 1).astype(jnp.int32),
        "live_count": draw_live_count(jax.random.fold_in(key_of[10], 71), 0),
        "send_group": draw_send_group(jax.random.fold_in(key_of[10], 71), 0),
        "recv_group": draw_recv_group(jax.random.fold_in(key_of[10], 71), 0),
    }


def reference(currents, basis_group, projection, filters, pair_src, pair_dst, pair_type, live_count, send_group, recv_group):
    device_rows = BPG * G_DEV
    labels = jnp.arange(G_DEV, dtype=jnp.int32)
    currents_dev = currents.reshape(READERS, device_rows, NT)
    pattern_dev = projection.reshape(READERS, device_rows, K)
    member_device = basis_group.reshape(READERS, device_rows)

    def project(inputs):
        series, pattern, member = inputs
        onehot = (member[:, None] == labels[None, :]).astype(jnp.float32)
        spread = series.astype(jnp.float32)[:, None, :] * onehot[:, :, None]
        return jnp.einsum("bk,bgt->gkt", pattern.astype(jnp.float32), spread, precision=lax.Precision.HIGHEST)

    signature = lax.map(project, (currents_dev, pattern_dev, member_device))
    signature = signature.reshape(GROUPS, K, NT).astype(jnp.bfloat16)

    rows = jnp.arange(READERS * FAR_DEV, dtype=jnp.int32)
    reader = rows // FAR_DEV
    slot = rows % FAR_DEV
    live = slot < live_count[reader]
    source = pair_src * G_DEV + send_group[pair_src, reader]
    target = pair_dst * G_DEV + recv_group[pair_dst, reader]
    delay_bucket = target * TYPES + pair_type

    def add_reader(store, inputs):
        source_row, bucket_row, live_row = inputs
        values = jnp.take(signature, source_row, axis=0).astype(jnp.float32)
        values = values * live_row.astype(jnp.float32)[:, None, None]
        return store.at[bucket_row].add(values), None

    store = jnp.zeros((GROUPS * TYPES, K, NT), dtype=jnp.float32)
    store, _ = lax.scan(add_reader, store, (source.reshape(READERS, FAR_DEV), delay_bucket.reshape(READERS, FAR_DEV), live.reshape(READERS, FAR_DEV)))
    store = store.reshape(GROUPS, TYPES, K, NT)

    times = jnp.arange(NT, dtype=jnp.int32)
    delay = times[None, :] - times[:, None]
    valid = (delay >= 0) & (delay < TAPS)
    lag_index = jnp.clip(delay, 0, TAPS - 1)
    toeplitz = jnp.take(filters.astype(jnp.float32), lag_index, axis=1)
    toeplitz = jnp.where(valid[None, :, :, None], toeplitz, jnp.zeros_like(toeplitz))
    incoming = jnp.einsum("gcks,cstk->gkt", store, toeplitz, precision=lax.Precision.HIGHEST)
    incoming = incoming.astype(jnp.bfloat16).reshape(READERS, G_DEV, K, NT)

    def disaggregate(inputs):
        pattern, member, arriving = inputs
        onehot = (member[:, None] == labels[None, :]).astype(jnp.float32)
        spread = jnp.einsum("bk,gkt->bgt", pattern.astype(jnp.float32), arriving.astype(jnp.float32), precision=lax.Precision.HIGHEST)
        return jnp.sum(spread * onehot[:, :, None], axis=1)

    field = lax.map(disaggregate, (pattern_dev, member_device, incoming))
    return field.reshape(BASIS, NT).astype(jnp.bfloat16)
```

```python
import functools

import jax
import jax.numpy as jnp
import numpy as np
from jax import lax
from jax.experimental import pallas as pl
from jax.experimental.pallas import tpu as pltpu
from jax.sharding import PartitionSpec as P

G_DEV = 2
LANES = 128
TABLE_ROWS = 16
BF16 = jnp.bfloat16
F32 = jnp.float32

VMEM = pl.BlockSpec(memory_space=pltpu.VMEM)
SMEM = pl.BlockSpec(memory_space=pltpu.SMEM)


def halves(table):
    high = table.astype(jnp.bfloat16)
    low = (table - high.astype(np.float64)).astype(jnp.bfloat16)
    return high, low


def wave_tables(steps):
    angle = np.pi * np.outer(np.arange(steps), np.arange(steps) + 0.5) / steps
    forward = np.concatenate([np.cos(angle), -np.sin(angle)], axis=1)
    inverse = forward.T / steps
    return halves(forward), halves(inverse)


def dot(a, b, dims=((1,), (0,))):
    return lax.dot_general(a, b, (dims, ((), ())), preferred_element_type=F32)


def member_column(group_row):
    rows = group_row.shape[1]
    return jnp.broadcast_to(group_row.astype(F32), (LANES, rows)).T[:, :1]


def project_kernel(
    readers,
    slots,
    position_ref,
    currents_ref,
    group_ref,
    projection_ref,
    src_ref,
    dst_ref,
    type_ref,
    live_ref,
    send_ref,
    recv_ref,
    out_ref,
):
    steps = currents_ref.shape[1]
    block = projection_ref.shape[1] // readers
    rows = out_ref.shape[1]
    me = position_ref[0]
    column = member_column(group_ref[...])
    series = currents_ref[...].astype(F32)
    spread = jnp.concatenate(
        [jnp.where(column == g, series, 0.0).astype(BF16) for g in range(G_DEV)], axis=1
    )
    signature = dot(projection_ref[...], spread, ((0,), (0,))).astype(BF16)
    for owner in range(readers):
        for g in range(G_DEV):
            out_ref[owner, pl.ds(g * block, block), :] = signature[
                owner * block : (owner + 1) * block, g * steps : (g + 1) * steps
            ]

    pack = max(1, LANES // slots)
    first = lax.rem(me, pack) * slots
    lane = lax.broadcasted_iota(jnp.int32, (TABLE_ROWS, LANES), 1)
    row = lax.broadcasted_iota(jnp.int32, (TABLE_ROWS, LANES), 0)
    live = live_ref[0]

    def add_slot(p, table):
        src = src_ref[p]
        dst = dst_ref[p]
        source = src * G_DEV + send_ref[src, me]
        target = dst * G_DEV + recv_ref[dst, me] + 1
        target = jnp.where(p < live, target, 0)
        value = jnp.where(row == 0, source, jnp.where(row == 1, target, type_ref[p]))
        return jnp.where(lane == first + p, value, table)

    table = lax.fori_loop(
        0, slots, add_slot, jnp.zeros((TABLE_ROWS, LANES), jnp.int32), unroll=slots <= 16
    )
    table = table.astype(F32).astype(BF16)
    for owner in range(readers):
        out_ref[owner, pl.ds(rows - TABLE_ROWS, TABLE_ROWS), :] = table


def filter_kernel(filters_ref, wave_ref, out_ref):
    types, taps, width = filters_ref.shape
    wave = wave_ref[...]
    for c in range(types):
        taps_c = filters_ref[c]
        out_ref[c] = dot(jnp.concatenate([taps_c, taps_c], axis=0), wave, ((0,), (0,)))


def split(value):
    high = value.astype(BF16)
    return high, (value - high.astype(F32)).astype(BF16)


def translate_kernel(
    readers,
    slots,
    block,
    position_ref,
    arrived_ref,
    response_ref,
    forward_ref,
    inverse_high_ref,
    inverse_low_ref,
    out_ref,
    order_ref,
    wave_ref,
    product_ref,
    result_ref,
):
    types = response_ref.shape[0]
    steps = inverse_high_ref.shape[1]
    groups = readers * G_DEV
    rows = G_DEV * block + TABLE_ROWS
    base = position_ref[0] * block

    for owner in range(readers):
        part = arrived_ref[pl.ds(owner * rows, G_DEV * block), :]
        order_ref[pl.ds(owner * G_DEV * block, G_DEV * block), :] = part.astype(F32)

    pack = max(1, LANES // slots)
    count = jnp.zeros((types * groups, groups), F32)
    bucket_row = lax.broadcasted_iota(jnp.int32, (types * groups, LANES), 0)
    group_row = lax.broadcasted_iota(jnp.int32, (groups, LANES), 0)
    for first in range(0, readers, pack):
        table = jnp.zeros((TABLE_ROWS, LANES), F32)
        for owner in range(first, min(first + pack, readers)):
            start = owner * rows + G_DEV * block
            table = table + arrived_ref[pl.ds(start, TABLE_ROWS), :].astype(F32)
        table = table.astype(jnp.int32)
        source, target, kind = table[0:1], table[1:2], table[2:3]
        bucket = jnp.where(target > 0, kind * groups + target - 1, -1)
        to_bucket = (bucket_row == bucket).astype(F32).astype(BF16)
        from_group = (group_row == source).astype(F32).astype(BF16)
        count = count + dot(to_bucket, from_group, ((1,), (1,)))
    count_high, count_low = split(count)
    if readers * slots > 256:
        count_parts = jnp.concatenate([count_high, count_high, count_low, count_low], axis=1)
    else:
        count_parts = jnp.concatenate([count_high, count_high], axis=1)

    forward = forward_ref[...]
    for k in range(block):
        signal = order_ref[pl.ds(k, groups, stride=block), :].astype(BF16)
        wave_ref[pl.ds(k * groups, groups), :] = signal
    signals = wave_ref[...]
    waves = dot(jnp.concatenate([signals, signals], axis=1), forward)
    for k in range(block):
        high, low = split(waves[k * groups : (k + 1) * groups])
        if readers * slots > 256:
            parts = jnp.concatenate([high, low, high, low], axis=0)
        else:
            parts = jnp.concatenate([high, low], axis=0)
        gathered = dot(count_parts, parts)
        real = jnp.zeros((groups, steps), F32)
        imag = jnp.zeros((groups, steps), F32)
        for c in range(types):
            response = response_ref[c, pl.ds(base + k, 1), :]
            response_real, response_imag = response[:, :steps], response[:, steps:]
            bucket = gathered[c * groups : (c + 1) * groups]
            bucket_real, bucket_imag = bucket[:, :steps], bucket[:, steps:]
            real = real + (bucket_real * response_real - bucket_imag * response_imag)
            imag = imag + (bucket_real * response_imag + bucket_imag * response_real)
        product_ref[pl.ds(k * groups, groups), pl.ds(0, steps)] = real
        product_ref[pl.ds(k * groups, groups), pl.ds(steps, steps)] = imag
    high, low = split(product_ref[...])
    inverse_high = inverse_high_ref[...]
    result_ref[...] = (
        dot(high, inverse_high) + dot(low, inverse_high) + dot(high, inverse_low_ref[...])
    )
    for g in range(groups):
        out_ref[pl.ds(g * block, block), :] = result_ref[
            pl.ds(g, block, stride=groups), :
        ].astype(BF16)


def field_kernel(readers, block, group_ref, projection_ref, incoming_ref, out_ref):
    column = member_column(group_ref[...])
    projection = projection_ref[...]
    field = None
    for g in range(G_DEV):
        incoming = jnp.concatenate(
            [
                incoming_ref[pl.ds((part * G_DEV + g) * block, block), :]
                for part in range(readers)
            ],
            axis=0,
        )
        term = dot(projection, incoming)
        field = term if g == 0 else jnp.where(column == g, term, field)
    out_ref[...] = field.astype(BF16)


def local(
    currents,
    basis_group,
    projection,
    filters,
    pair_src,
    pair_dst,
    pair_type,
    live_count,
    send_group,
    recv_group,
):
    readers = lax.axis_size("grp")
    spans = lax.axis_size("dir")
    steps = currents.shape[1]
    basis, width = projection.shape
    types, taps, _ = filters.shape
    slots = pair_src.shape[0]
    block = width // readers
    groups = readers * G_DEV
    rows = G_DEV * block + TABLE_ROWS
    position = lax.axis_index("grp").astype(jnp.int32).reshape(1)
    (forward_high, forward_low), (inverse_high, inverse_low) = wave_tables(steps)
    group_row = basis_group.reshape(1, basis)

    outgoing = pl.pallas_call(
        functools.partial(project_kernel, readers, slots),
        out_shape=jax.ShapeDtypeStruct((readers, rows, steps), BF16),
        in_specs=[SMEM, VMEM, VMEM, VMEM, SMEM, SMEM, SMEM, SMEM, SMEM, SMEM],
        out_specs=VMEM,
    )(
        position,
        currents,
        group_row,
        projection,
        pair_src,
        pair_dst,
        pair_type,
        live_count,
        send_group,
        recv_group,
    )
    arrived = lax.all_to_all(outgoing, "grp", split_axis=0, concat_axis=0, tiled=True)
    response = pl.pallas_call(
        filter_kernel,
        out_shape=jax.ShapeDtypeStruct((types, width, 2 * steps), F32),
        in_specs=[VMEM, VMEM],
        out_specs=VMEM,
        cost_estimate=pl.CostEstimate(
            flops=8 * types * width * taps * steps, bytes_accessed=2**21, transcendentals=0
        ),
    )(filters, np.concatenate([forward_high[:taps], forward_low[:taps]], axis=0))
    incoming = pl.pallas_call(
        functools.partial(translate_kernel, readers, slots, block),
        out_shape=jax.ShapeDtypeStruct((groups * block, steps), BF16),
        in_specs=[SMEM, VMEM, VMEM, VMEM, VMEM, VMEM],
        out_specs=VMEM,
        scratch_shapes=[
            pltpu.VMEM((groups * block, steps), F32),
            pltpu.VMEM((groups * block, steps), BF16),
            pltpu.VMEM((groups * block, 2 * steps), F32),
            pltpu.VMEM((groups * block, steps), F32),
        ],
    )(
        position,
        arrived.reshape(readers * rows, steps),
        response,
        np.concatenate([forward_high, forward_low], axis=0),
        inverse_high,
        inverse_low,
    )
    incoming = incoming.reshape(readers, G_DEV * block, steps)
    own = lax.all_to_all(incoming, "grp", split_axis=0, concat_axis=0, tiled=True)
    term = pl.pallas_call(
        functools.partial(field_kernel, readers, block),
        out_shape=jax.ShapeDtypeStruct((basis, steps), BF16),
        in_specs=[VMEM, VMEM, VMEM],
        out_specs=VMEM,
    )(group_row, projection, own.reshape(groups * block, steps))

    sums = [term.astype(F32)]
    for other in range(1, spans):
        pairs = [(d, d ^ other) for d in range(spans)]
        sums.append(lax.ppermute(term, "dir", pairs).astype(F32))
    while len(sums) > 1:
        sums = [sums[i] + sums[i + 1] for i in range(0, len(sums), 2)]
    return sums[0].astype(BF16)


def solution(mesh):
    return jax.shard_map(
        local,
        mesh=mesh,
        in_specs=(
            P("grp", None),
            P("grp"),
            P("grp", "dir"),
            P(None, None, "dir"),
            P("grp"),
            P("grp"),
            P("grp"),
            P("grp"),
            P(),
            P(),
        ),
        out_specs=P("grp", None),
        check_vma=False,
    )
```

```python
import functools

import jax
import jax.numpy as jnp
import numpy as np
from jax import lax
from jax.experimental import pallas as pl
from jax.experimental.pallas import tpu as pltpu
from jax.sharding import PartitionSpec as P

G_DEV = 2
LANES = 128
TABLE_ROWS = 8
BF16 = jnp.bfloat16
F32 = jnp.float32

VMEM = pl.BlockSpec(memory_space=pltpu.VMEM)
FAR = pl.BlockSpec(memory_space=pl.ANY)
PARAMS = pltpu.CompilerParams(vmem_limit_bytes=16 * 2**20)


def near(value):
    return pltpu.with_memory_space_constraint(value, pltpu.VMEM)


def halves(table):
    high = table.astype(jnp.bfloat16)
    low = (table - high.astype(np.float64)).astype(jnp.bfloat16)
    return high, low


def wave_tables(steps):
    angle = np.pi * np.outer(np.arange(steps), np.arange(steps) + 0.5) / steps
    forward = np.concatenate([np.cos(angle), -np.sin(angle)], axis=1)
    inverse = forward.T / steps
    return halves(forward), halves(inverse)


def dot(a, b, dims=((1,), (0,))):
    return lax.dot_general(a, b, (dims, ((), ())), preferred_element_type=F32)


def project_kernel(
    readers,
    slots,
    currents_hbm,
    group_hbm,
    projection_hbm,
    src_hbm,
    dst_hbm,
    type_hbm,
    live_hbm,
    send_hbm,
    recv_hbm,
    out_ref,
    currents_ref,
    group_ref,
    projection_ref,
    src_ref,
    dst_ref,
    type_ref,
    live_ref,
    send_ref,
    recv_ref,
    sems,
):
    wide = [
        pltpu.make_async_copy(source, target, sems.at[i])
        for i, (source, target) in enumerate(
            [(projection_hbm, projection_ref), (currents_hbm, currents_ref), (group_hbm, group_ref)]
        )
    ]
    small = [
        pltpu.make_async_copy(source, target, sems.at[len(wide) + i])
        for i, (source, target) in enumerate(
            [
                (src_hbm, src_ref),
                (dst_hbm, dst_ref),
                (type_hbm, type_ref),
                (live_hbm, live_ref),
                (send_hbm, send_ref),
                (recv_hbm, recv_ref),
            ]
        )
    ]
    for copy in wide + small:
        copy.start()

    steps = currents_ref.shape[1]
    block = projection_ref.shape[1] // readers
    rows = out_ref.shape[1]
    me = lax.axis_index("grp")
    pack = max(1, LANES // slots)
    first = lax.rem(me, pack) * slots
    lane = lax.broadcasted_iota(jnp.int32, (TABLE_ROWS, LANES), 1)
    row = lax.broadcasted_iota(jnp.int32, (TABLE_ROWS, LANES), 0)
    for copy in small + wide:
        copy.wait()
    live = live_ref[0, 0]

    def add_slot(p, table):
        src = src_ref[p]
        dst = dst_ref[p]
        source = src * G_DEV + send_ref[src, me]
        target = dst * G_DEV + recv_ref[dst, me] + 1
        target = jnp.where(p < live, target, 0)
        value = jnp.where(row == 0, source, jnp.where(row == 1, target, type_ref[p]))
        return jnp.where(lane == first + p, value, table)

    table = lax.fori_loop(
        0, slots, add_slot, jnp.zeros((TABLE_ROWS, LANES), jnp.int32), unroll=slots <= 16
    )
    table = table.astype(F32).astype(BF16)
    for owner in range(readers):
        out_ref[owner, pl.ds(rows - TABLE_ROWS, TABLE_ROWS), :] = table

    pattern = projection_ref[...].T
    series = currents_ref[...]
    for g in range(G_DEV):
        member = (group_ref[...] == g).astype(F32).astype(BF16)
        signature = dot(pattern * member, series).astype(BF16)
        for owner in range(readers):
            out_ref[owner, pl.ds(g * block, block), :] = signature[
                owner * block : (owner + 1) * block
            ]


def filter_kernel(group_ref, filters_ref, wave_ref, out_ref, column_ref):
    types, taps, width = filters_ref.shape
    wave = wave_ref[...]
    for c in range(types):
        taps_c = filters_ref[c]
        out_ref[c] = dot(jnp.concatenate([taps_c, taps_c], axis=0), wave, ((0,), (0,)))
    column_ref[...] = jnp.broadcast_to(
        group_ref[...].astype(F32), (LANES, group_ref.shape[1])
    ).T


def split(value):
    high = value.astype(BF16)
    return high, (value - high.astype(F32)).astype(BF16)


def translate_kernel(
    readers,
    slots,
    block,
    arrived_ref,
    response_ref,
    forward_ref,
    inverse_high_ref,
    inverse_low_ref,
    out_ref,
    order_ref,
    wave_ref,
    product_ref,
    result_ref,
):
    types = response_ref.shape[0]
    steps = inverse_high_ref.shape[1]
    groups = readers * G_DEV
    rows = G_DEV * block + TABLE_ROWS
    base = lax.axis_index("grp") * block

    for owner in range(readers):
        part = arrived_ref[pl.ds(owner * rows, G_DEV * block), :]
        order_ref[pl.ds(owner * G_DEV * block, G_DEV * block), :] = part.astype(F32)

    pack = max(1, LANES // slots)
    count = jnp.zeros((types * groups, groups), F32)
    bucket_row = lax.broadcasted_iota(jnp.int32, (types * groups, LANES), 0)
    group_row = lax.broadcasted_iota(jnp.int32, (groups, LANES), 0)
    for first in range(0, readers, pack):
        table = jnp.zeros((TABLE_ROWS, LANES), F32)
        for owner in range(first, min(first + pack, readers)):
            start = owner * rows + G_DEV * block
            table = table + arrived_ref[pl.ds(start, TABLE_ROWS), :].astype(F32)
        table = table.astype(jnp.int32)
        source, target, kind = table[0:1], table[1:2], table[2:3]
        bucket = jnp.where(target > 0, kind * groups + target - 1, -1)
        to_bucket = (bucket_row == bucket).astype(F32).astype(BF16)
        from_group = (group_row == source).astype(F32).astype(BF16)
        count = count + dot(to_bucket, from_group, ((1,), (1,)))
    count_high, count_low = split(count)
    if readers * slots > 256:
        count_parts = jnp.concatenate([count_high, count_high, count_low, count_low], axis=1)
    else:
        count_parts = jnp.concatenate([count_high, count_high], axis=1)

    forward = forward_ref[...]
    for k in range(block):
        signal = order_ref[pl.ds(k, groups, stride=block), :].astype(BF16)
        wave_ref[pl.ds(k * groups, groups), :] = signal
    signals = wave_ref[...]
    waves = dot(jnp.concatenate([signals, signals], axis=1), forward)
    for k in range(block):
        high, low = split(waves[k * groups : (k + 1) * groups])
        if readers * slots > 256:
            parts = jnp.concatenate([high, low, high, low], axis=0)
        else:
            parts = jnp.concatenate([high, low], axis=0)
        gathered = dot(count_parts, parts)
        real = jnp.zeros((groups, steps), F32)
        imag = jnp.zeros((groups, steps), F32)
        for c in range(types):
            response = response_ref[c, pl.ds(base + k, 1), :]
            response_real, response_imag = response[:, :steps], response[:, steps:]
            bucket = gathered[c * groups : (c + 1) * groups]
            bucket_real, bucket_imag = bucket[:, :steps], bucket[:, steps:]
            real = real + (bucket_real * response_real - bucket_imag * response_imag)
            imag = imag + (bucket_real * response_imag + bucket_imag * response_real)
        product_ref[pl.ds(k * groups, groups), pl.ds(0, steps)] = real
        product_ref[pl.ds(k * groups, groups), pl.ds(steps, steps)] = imag
    high, low = split(product_ref[...])
    inverse_high = inverse_high_ref[...]
    result_ref[...] = (
        dot(high, inverse_high) + dot(low, inverse_high) + dot(high, inverse_low_ref[...])
    )
    for g in range(groups):
        out_ref[pl.ds(g * block, block), :] = result_ref[
            pl.ds(g, block, stride=groups), :
        ].astype(BF16)


def field_kernel(readers, block, column_ref, projection_ref, incoming_ref, out_ref):
    column = column_ref[:, :1]
    projection = projection_ref[...]
    field = None
    for g in range(G_DEV):
        incoming = jnp.concatenate(
            [
                incoming_ref[pl.ds((part * G_DEV + g) * block, block), :]
                for part in range(readers)
            ],
            axis=0,
        )
        term = dot(projection, incoming)
        field = term if g == 0 else jnp.where(column == g, term, field)
    out_ref[...] = field.astype(BF16)


def local(
    currents,
    basis_group,
    projection,
    filters,
    pair_src,
    pair_dst,
    pair_type,
    live_count,
    send_group,
    recv_group,
):
    readers = lax.axis_size("grp")
    spans = lax.axis_size("dir")
    steps = currents.shape[1]
    basis, width = projection.shape
    types, taps, _ = filters.shape
    slots = pair_src.shape[0]
    block = width // readers
    groups = readers * G_DEV
    rows = G_DEV * block + TABLE_ROWS
    (forward_high, forward_low), (inverse_high, inverse_low) = wave_tables(steps)
    group_row = basis_group.reshape(1, basis)

    inputs = (
        currents,
        group_row,
        projection,
        pair_src,
        pair_dst,
        pair_type,
        live_count.reshape(1, 1),
        send_group,
        recv_group,
    )
    outgoing = pl.pallas_call(
        functools.partial(project_kernel, readers, slots),
        out_shape=jax.ShapeDtypeStruct((readers, rows, steps), BF16),
        in_specs=[FAR] * len(inputs),
        out_specs=VMEM,
        scratch_shapes=[pltpu.VMEM(x.shape, x.dtype) for x in inputs[:3]]
        + [pltpu.SMEM(x.shape, x.dtype) for x in inputs[3:]]
        + [pltpu.SemaphoreType.DMA((len(inputs),))],
    )(*inputs)
    arrived = lax.all_to_all(outgoing, "grp", split_axis=0, concat_axis=0, tiled=True)
    response, column = pl.pallas_call(
        filter_kernel,
        out_shape=(
            pltpu.VMEM((types, width, 2 * steps), F32),
            pltpu.VMEM((basis, LANES), F32),
        ),
        in_specs=[VMEM, VMEM, VMEM],
        out_specs=(VMEM, VMEM),
        compiler_params=PARAMS,
        cost_estimate=pl.CostEstimate(
            flops=8 * types * width * taps * steps, bytes_accessed=2**21, transcendentals=0
        ),
    )(group_row, filters, np.concatenate([forward_high[:taps], forward_low[:taps]], axis=0))
    incoming = pl.pallas_call(
        functools.partial(translate_kernel, readers, slots, block),
        out_shape=pltpu.VMEM((groups * block, steps), BF16),
        in_specs=[VMEM, VMEM, VMEM, VMEM, VMEM],
        out_specs=VMEM,
        compiler_params=PARAMS,
        scratch_shapes=[
            pltpu.VMEM((groups * block, steps), F32),
            pltpu.VMEM((groups * block, steps), BF16),
            pltpu.VMEM((groups * block, 2 * steps), F32),
            pltpu.VMEM((groups * block, steps), F32),
        ],
    )(
        near(arrived.reshape(readers * rows, steps)),
        near(response),
        near(jnp.asarray(np.concatenate([forward_high, forward_low], axis=0))),
        near(jnp.asarray(inverse_high)),
        near(jnp.asarray(inverse_low)),
    )
    incoming = incoming.reshape(readers, G_DEV * block, steps)
    own = lax.all_to_all(incoming, "grp", split_axis=0, concat_axis=0, tiled=True)
    term = pl.pallas_call(
        functools.partial(field_kernel, readers, block),
        out_shape=pltpu.VMEM((basis, steps), BF16),
        in_specs=[VMEM, VMEM, VMEM],
        out_specs=VMEM,
        compiler_params=PARAMS,
    )(near(column), near(projection), near(own.reshape(groups * block, steps)))

    sums = [term.astype(F32)]
    for other in range(1, spans):
        pairs = [(d, d ^ other) for d in range(spans)]
        sums.append(lax.ppermute(term, "dir", pairs).astype(F32))
    while len(sums) > 1:
        sums = [sums[i] + sums[i + 1] for i in range(0, len(sums), 2)]
    return sums[0].astype(BF16)


def solution(mesh):
    return jax.shard_map(
        local,
        mesh=mesh,
        in_specs=(
            P("grp", None),
            P("grp"),
            P("grp", "dir"),
            P(None, None, "dir"),
            P("grp"),
            P("grp"),
            P("grp"),
            P("grp"),
            P(),
            P(),
        ),
        out_specs=P("grp", None),
        check_vma=False,
    )
```

```python
import functools

import jax
import jax.numpy as jnp
import numpy as np
from jax import lax
from jax.experimental import pallas as pl
from jax.experimental.pallas import tpu as pltpu
from jax.sharding import PartitionSpec as P

G_DEV = 2
LANES = 128
TABLE_ROWS = 8
BF16 = jnp.bfloat16
F32 = jnp.float32

VMEM = pl.BlockSpec(memory_space=pltpu.VMEM)
FAR = pl.BlockSpec(memory_space=pl.ANY)
PARAMS = pltpu.CompilerParams(vmem_limit_bytes=16 * 2**20)


def near(value):
    return pltpu.with_memory_space_constraint(value, pltpu.VMEM)


def halves(table):
    high = table.astype(jnp.bfloat16)
    low = (table - high.astype(np.float64)).astype(jnp.bfloat16)
    return high, low


def wave_tables(steps):
    angle = np.pi * np.outer(np.arange(steps), np.arange(steps) + 0.5) / steps
    forward = np.concatenate([np.cos(angle), -np.sin(angle)], axis=1)
    inverse = forward.T / steps
    return halves(forward), halves(inverse)


def dot(a, b, dims=((1,), (0,))):
    return lax.dot_general(a, b, (dims, ((), ())), preferred_element_type=F32)


def project_kernel(
    readers,
    slots,
    currents_hbm,
    group_hbm,
    projection_hbm,
    src_hbm,
    dst_hbm,
    type_hbm,
    live_hbm,
    send_hbm,
    recv_hbm,
    out_ref,
    currents_ref,
    group_ref,
    projection_ref,
    src_ref,
    dst_ref,
    type_ref,
    live_ref,
    send_ref,
    recv_ref,
    sems,
):
    wide = [
        pltpu.make_async_copy(source, target, sems.at[i])
        for i, (source, target) in enumerate(
            [(projection_hbm, projection_ref), (currents_hbm, currents_ref), (group_hbm, group_ref)]
        )
    ]
    small = [
        pltpu.make_async_copy(source, target, sems.at[len(wide) + i])
        for i, (source, target) in enumerate(
            [
                (src_hbm, src_ref),
                (dst_hbm, dst_ref),
                (type_hbm, type_ref),
                (live_hbm, live_ref),
                (send_hbm, send_ref),
                (recv_hbm, recv_ref),
            ]
        )
    ]
    for copy in wide + small:
        copy.start()

    steps = currents_ref.shape[1]
    block = projection_ref.shape[1] // readers
    rows = out_ref.shape[1]
    me = lax.axis_index("grp")
    pack = max(1, LANES // slots)
    first = lax.rem(me, pack) * slots
    lane = lax.broadcasted_iota(jnp.int32, (TABLE_ROWS, LANES), 1)
    row = lax.broadcasted_iota(jnp.int32, (TABLE_ROWS, LANES), 0)
    for copy in small + wide:
        copy.wait()
    live = live_ref[0, 0]

    def add_slot(p, table):
        src = src_ref[p]
        dst = dst_ref[p]
        source = src * G_DEV + send_ref[src, me]
        target = dst * G_DEV + recv_ref[dst, me] + 1
        target = jnp.where(p < live, target, 0)
        value = jnp.where(row == 0, source, jnp.where(row == 1, target, type_ref[p]))
        return jnp.where(lane == first + p, value, table)

    table = lax.fori_loop(
        0, slots, add_slot, jnp.zeros((TABLE_ROWS, LANES), jnp.int32), unroll=slots <= 16
    )
    table = table.astype(F32).astype(BF16)
    for owner in range(readers):
        out_ref[owner, pl.ds(rows - TABLE_ROWS, TABLE_ROWS), :] = table

    pattern = projection_ref[...].T
    series = currents_ref[...]
    for g in range(G_DEV):
        member = (group_ref[...] == g).astype(F32).astype(BF16)
        signature = dot(pattern * member, series).astype(BF16)
        for owner in range(readers):
            out_ref[owner, pl.ds(g * block, block), :] = signature[
                owner * block : (owner + 1) * block
            ]


def filter_kernel(group_ref, filters_ref, wave_ref, out_ref, column_ref):
    types, taps, width = filters_ref.shape
    wave = wave_ref[...]
    for c in range(types):
        taps_c = filters_ref[c]
        out_ref[c] = dot(jnp.concatenate([taps_c, taps_c], axis=0), wave, ((0,), (0,)))
    column_ref[...] = jnp.broadcast_to(
        group_ref[...].astype(F32), (LANES, group_ref.shape[1])
    ).T


def split(value):
    high = value.astype(BF16)
    return high, (value - high.astype(F32)).astype(BF16)


def translate_kernel(
    readers,
    slots,
    block,
    arrived_ref,
    response_ref,
    forward_ref,
    inverse_high_ref,
    inverse_low_ref,
    out_ref,
    order_ref,
    wave_ref,
    product_ref,
    result_ref,
):
    types = response_ref.shape[0]
    steps = inverse_high_ref.shape[1]
    groups = readers * G_DEV
    rows = G_DEV * block + TABLE_ROWS
    base = lax.axis_index("grp") * block

    for owner in range(readers):
        part = arrived_ref[pl.ds(owner * rows, G_DEV * block), :]
        order_ref[pl.ds(owner * G_DEV * block, G_DEV * block), :] = part.astype(F32)

    pack = max(1, LANES // slots)
    count = jnp.zeros((types * groups, groups), F32)
    bucket_row = lax.broadcasted_iota(jnp.int32, (types * groups, LANES), 0)
    group_row = lax.broadcasted_iota(jnp.int32, (groups, LANES), 0)
    for first in range(0, readers, pack):
        table = jnp.zeros((TABLE_ROWS, LANES), F32)
        for owner in range(first, min(first + pack, readers)):
            start = owner * rows + G_DEV * block
            table = table + arrived_ref[pl.ds(start, TABLE_ROWS), :].astype(F32)
        table = table.astype(jnp.int32)
        source, target, kind = table[0:1], table[1:2], table[2:3]
        bucket = jnp.where(target > 0, kind * groups + target - 1, -1)
        to_bucket = (bucket_row == bucket).astype(F32).astype(BF16)
        from_group = (group_row == source).astype(F32).astype(BF16)
        count = count + dot(to_bucket, from_group, ((1,), (1,)))
    count_high, count_low = split(count)
    if readers * slots > 256:
        count_parts = jnp.concatenate([count_high, count_high, count_low, count_low], axis=1)
    else:
        count_parts = jnp.concatenate([count_high, count_high], axis=1)

    forward = forward_ref[...]
    for k in range(block):
        signal = order_ref[pl.ds(k, groups, stride=block), :].astype(BF16)
        wave_ref[pl.ds(k * groups, groups), :] = signal
    signals = wave_ref[...]
    waves = dot(jnp.concatenate([signals, signals], axis=1), forward)
    for k in range(block):
        high, low = split(waves[k * groups : (k + 1) * groups])
        if readers * slots > 256:
            parts = jnp.concatenate([high, low, high, low], axis=0)
        else:
            parts = jnp.concatenate([high, low], axis=0)
        gathered = dot(count_parts, parts)
        real = jnp.zeros((groups, steps), F32)
        imag = jnp.zeros((groups, steps), F32)
        for c in range(types):
            response = response_ref[c, pl.ds(base + k, 1), :]
            response_real, response_imag = response[:, :steps], response[:, steps:]
            bucket = gathered[c * groups : (c + 1) * groups]
            bucket_real, bucket_imag = bucket[:, :steps], bucket[:, steps:]
            real = real + (bucket_real * response_real - bucket_imag * response_imag)
            imag = imag + (bucket_real * response_imag + bucket_imag * response_real)
        product_ref[pl.ds(k * groups, groups), pl.ds(0, steps)] = real
        product_ref[pl.ds(k * groups, groups), pl.ds(steps, steps)] = imag
    high, low = split(product_ref[...])
    inverse_high = inverse_high_ref[...]
    result_ref[...] = (
        dot(high, inverse_high) + dot(low, inverse_high) + dot(high, inverse_low_ref[...])
    )
    copies = out_ref.shape[0] // (groups * block)
    for g in range(groups):
        part = result_ref[pl.ds(g, block, stride=groups), :].astype(BF16)
        owner, own = divmod(g, G_DEV)
        for copy in range(copies):
            start = ((copy * readers + owner) * G_DEV + own) * block
            out_ref[pl.ds(start, block), :] = part


def field_kernel(readers, block, column_ref, own_ref, other_ref, incoming_ref, out_ref):
    column = column_ref[:, :1]
    outer = lax.axis_size("outer")
    here = lax.axis_index("outer")
    own = own_ref[...]
    if outer == 1:
        projection = own
    else:
        other = other_ref[...]
        projection = jnp.concatenate(
            [jnp.where(here == x, own, other) for x in range(outer)], axis=1
        )
    field = None
    for g in range(G_DEV):
        incoming = jnp.concatenate(
            [
                incoming_ref[pl.ds(((x * readers + part) * G_DEV + g) * block, block), :]
                for x in range(outer)
                for part in range(readers)
            ],
            axis=0,
        )
        term = dot(projection, incoming)
        field = term if g == 0 else jnp.where(column == g, term, field)
    out_ref[...] = field


def local(
    currents,
    basis_group,
    projection,
    filters,
    pair_src,
    pair_dst,
    pair_type,
    live_count,
    send_group,
    recv_group,
):
    readers = lax.axis_size("grp")
    outer = lax.axis_size("outer")
    inner = lax.axis_size("inner")
    steps = currents.shape[1]
    basis, width = projection.shape
    types, taps, _ = filters.shape
    slots = pair_src.shape[0]
    block = width // readers
    groups = readers * G_DEV
    rows = G_DEV * block + TABLE_ROWS
    (forward_high, forward_low), (inverse_high, inverse_low) = wave_tables(steps)
    group_row = basis_group.reshape(1, basis)

    inputs = (
        currents,
        group_row,
        projection,
        pair_src,
        pair_dst,
        pair_type,
        live_count.reshape(1, 1),
        send_group,
        recv_group,
    )
    outgoing = pl.pallas_call(
        functools.partial(project_kernel, readers, slots),
        out_shape=jax.ShapeDtypeStruct((readers, rows, steps), BF16),
        in_specs=[FAR] * len(inputs),
        out_specs=VMEM,
        scratch_shapes=[pltpu.VMEM(x.shape, x.dtype) for x in inputs[:3]]
        + [pltpu.SMEM(x.shape, x.dtype) for x in inputs[3:]]
        + [pltpu.SemaphoreType.DMA((len(inputs),))],
    )(*inputs)
    arrived = lax.all_to_all(outgoing, "grp", split_axis=0, concat_axis=0, tiled=True)
    partner = lax.ppermute(projection, "outer", [(0, 1), (1, 0)])
    response, column = pl.pallas_call(
        filter_kernel,
        out_shape=(
            pltpu.VMEM((types, width, 2 * steps), F32),
            pltpu.VMEM((basis, LANES), F32),
        ),
        in_specs=[VMEM, VMEM, VMEM],
        out_specs=(VMEM, VMEM),
        compiler_params=PARAMS,
        cost_estimate=pl.CostEstimate(
            flops=8 * types * width * taps * steps, bytes_accessed=2**21, transcendentals=0
        ),
    )(group_row, filters, np.concatenate([forward_high[:taps], forward_low[:taps]], axis=0))
    arrived, partner = lax.optimization_barrier((arrived, partner))
    incoming = pl.pallas_call(
        functools.partial(translate_kernel, readers, slots, block),
        out_shape=pltpu.VMEM((outer * groups * block, steps), BF16),
        in_specs=[VMEM, VMEM, VMEM, VMEM, VMEM],
        out_specs=VMEM,
        compiler_params=PARAMS,
        scratch_shapes=[
            pltpu.VMEM((groups * block, steps), F32),
            pltpu.VMEM((groups * block, steps), BF16),
            pltpu.VMEM((groups * block, 2 * steps), F32),
            pltpu.VMEM((groups * block, steps), F32),
        ],
    )(
        near(arrived.reshape(readers * rows, steps)),
        near(response),
        near(jnp.asarray(np.concatenate([forward_high, forward_low], axis=0))),
        near(jnp.asarray(inverse_high)),
        near(jnp.asarray(inverse_low)),
    )
    incoming = incoming.reshape(outer * readers, G_DEV * block, steps)
    own = lax.all_to_all(incoming, ("outer", "grp"), split_axis=0, concat_axis=0, tiled=True)
    term = pl.pallas_call(
        functools.partial(field_kernel, readers, block),
        out_shape=pltpu.VMEM((basis, steps), F32),
        in_specs=[VMEM, VMEM, VMEM, VMEM],
        out_specs=VMEM,
        compiler_params=PARAMS,
    )(
        near(column),
        near(projection),
        near(partner),
        near(own.reshape(outer * groups * block, steps)),
    )
    total = term
    if inner > 1:
        total = term + lax.ppermute(term, "inner", [(0, 1), (1, 0)])
    return total.astype(BF16)


def solution(mesh):
    readers, spans = mesh.devices.shape
    split_mesh = jax.sharding.Mesh(
        mesh.devices.reshape(readers, spans // 2, 2), ("grp", "outer", "inner")
    )
    return jax.shard_map(
        local,
        mesh=split_mesh,
        in_specs=(
            P("grp", None),
            P("grp"),
            P("grp", ("outer", "inner")),
            P(None, None, ("outer", "inner")),
            P("grp"),
            P("grp"),
            P("grp"),
            P("grp"),
            P(),
            P(),
        ),
        out_specs=P("grp", None),
        check_vma=False,
    )
```

```python
import functools
import math

import jax
import jax.numpy as jnp
import numpy as np
from jax import lax
from jax.experimental import pallas as pl
from jax.experimental.pallas import tpu as pltpu
from jax.sharding import PartitionSpec as P

G_DEV = 2
LANES = 128
TABLE_ROWS = 8
BF16 = jnp.bfloat16
F32 = jnp.float32

VMEM = pl.BlockSpec(memory_space=pltpu.VMEM)
FAR = pl.BlockSpec(memory_space=pl.ANY)
PARAMS = pltpu.CompilerParams(vmem_limit_bytes=16 * 2**20)


def near(value):
    return pltpu.with_memory_space_constraint(value, pltpu.VMEM)


def halves(table):
    high = table.astype(jnp.bfloat16)
    low = (table - high.astype(np.float64)).astype(jnp.bfloat16)
    return high, low


def wave_tables(steps):
    angle = np.pi * np.outer(np.arange(steps), np.arange(steps) + 0.5) / steps
    forward = np.concatenate([np.cos(angle), -np.sin(angle)], axis=1)
    inverse = forward.T / steps
    return halves(forward), halves(inverse)


def dot(a, b, dims=((1,), (0,))):
    return lax.dot_general(a, b, (dims, ((), ())), preferred_element_type=F32)


def project_kernel(
    readers,
    slots,
    currents_hbm,
    group_hbm,
    projection_hbm,
    src_hbm,
    dst_hbm,
    type_hbm,
    live_hbm,
    send_hbm,
    recv_hbm,
    out_ref,
    currents_ref,
    group_ref,
    projection_ref,
    src_ref,
    dst_ref,
    type_ref,
    live_ref,
    send_ref,
    recv_ref,
    sems,
):
    wide = [
        pltpu.make_async_copy(source, target, sems.at[i])
        for i, (source, target) in enumerate(
            [(projection_hbm, projection_ref), (currents_hbm, currents_ref), (group_hbm, group_ref)]
        )
    ]
    small = [
        pltpu.make_async_copy(source, target, sems.at[len(wide) + i])
        for i, (source, target) in enumerate(
            [
                (src_hbm, src_ref),
                (dst_hbm, dst_ref),
                (type_hbm, type_ref),
                (live_hbm, live_ref),
                (send_hbm, send_ref),
                (recv_hbm, recv_ref),
            ]
        )
    ]
    for copy in wide + small:
        copy.start()

    steps = currents_ref.shape[1]
    block = projection_ref.shape[1] // readers
    rows = out_ref.shape[1]
    me = lax.axis_index("grp")
    pack = max(1, LANES // slots)
    first = lax.rem(me, pack) * slots
    lane = lax.broadcasted_iota(jnp.int32, (TABLE_ROWS, LANES), 1)
    row = lax.broadcasted_iota(jnp.int32, (TABLE_ROWS, LANES), 0)
    for copy in small + wide:
        copy.wait()
    live = live_ref[0, 0]

    def add_slot(p, table):
        src = src_ref[p]
        dst = dst_ref[p]
        source = src * G_DEV + send_ref[src, me]
        target = dst * G_DEV + recv_ref[dst, me] + 1
        target = jnp.where(p < live, target, 0)
        value = jnp.where(row == 0, source, jnp.where(row == 1, target, type_ref[p]))
        return jnp.where(lane == first + p, value, table)

    table = lax.fori_loop(
        0, slots, add_slot, jnp.zeros((TABLE_ROWS, LANES), jnp.int32), unroll=slots <= 16
    )
    table = table.astype(F32).astype(BF16)
    for owner in range(readers):
        out_ref[owner, pl.ds(rows - TABLE_ROWS, TABLE_ROWS), :] = table

    pattern = projection_ref[...].T
    series = currents_ref[...]
    for g in range(G_DEV):
        member = (group_ref[...] == g).astype(F32).astype(BF16)
        signature = dot(pattern * member, series).astype(BF16)
        for owner in range(readers):
            out_ref[owner, pl.ds(g * block, block), :] = signature[
                owner * block : (owner + 1) * block
            ]


def filter_kernel(group_ref, filters_ref, wave_ref, out_ref, column_ref):
    types, taps, width = filters_ref.shape
    wave = wave_ref[...]
    for c in range(types):
        taps_c = filters_ref[c]
        out_ref[c] = dot(jnp.concatenate([taps_c, taps_c], axis=0), wave, ((0,), (0,)))
    column_ref[...] = jnp.broadcast_to(
        group_ref[...].astype(F32), (LANES, group_ref.shape[1])
    ).T


def split(value):
    high = value.astype(BF16)
    return high, (value - high.astype(F32)).astype(BF16)


def translate_kernel(
    readers,
    slots,
    block,
    arrived_ref,
    response_ref,
    forward_ref,
    inverse_high_ref,
    inverse_low_ref,
    out_ref,
    order_ref,
    wave_ref,
    product_ref,
    result_ref,
):
    types = response_ref.shape[0]
    steps = inverse_high_ref.shape[1]
    groups = readers * G_DEV
    rows = G_DEV * block + TABLE_ROWS
    base = lax.axis_index("grp") * block

    for owner in range(readers):
        part = arrived_ref[pl.ds(owner * rows, G_DEV * block), :]
        order_ref[pl.ds(owner * G_DEV * block, G_DEV * block), :] = part.astype(F32)

    chunk = math.gcd(block, max(1, LANES // groups))
    span = chunk * groups
    pack = max(1, LANES // slots)
    count = jnp.zeros((types * groups, 2 * span), F32)
    bucket_row = lax.broadcasted_iota(jnp.int32, (types * groups, LANES), 0)
    group_row = lax.broadcasted_iota(jnp.int32, (groups, LANES), 0)
    for first in range(0, readers, pack):
        table = jnp.zeros((TABLE_ROWS, LANES), F32)
        for owner in range(first, min(first + pack, readers)):
            start = owner * rows + G_DEV * block
            table = table + arrived_ref[pl.ds(start, TABLE_ROWS), :].astype(F32)
        table = table.astype(jnp.int32)
        source, target, kind = table[0:1], table[1:2], table[2:3]
        bucket = jnp.where(target > 0, kind * groups + target - 1, -1)
        to_bucket = (bucket_row == bucket).astype(F32).astype(BF16)
        from_group = (group_row == source).astype(F32).astype(BF16)
        from_group = jnp.concatenate([from_group] * (2 * chunk), axis=0)
        count = count + dot(to_bucket, from_group, ((1,), (1,)))
    column = lax.broadcasted_iota(jnp.int32, (1, 2 * span), 1)
    column = jnp.where(column >= span, column - span, column)
    counts = []
    for i in range(chunk):
        own = (column >= i * groups) & (column < (i + 1) * groups)
        counts.append(count * own.astype(F32))
    counts = split(jnp.concatenate(counts, axis=0))
    if readers * slots <= 256:
        counts = counts[:1]

    forward = forward_ref[...]
    signals = order_ref[...].reshape(groups, block, steps)
    signals = jnp.swapaxes(signals, 0, 1).reshape(groups * block, steps).astype(BF16)
    waves = dot(jnp.concatenate([signals, signals], axis=1), forward)
    for first in range(0, block, chunk):
        parts = jnp.concatenate(split(waves[first * groups : first * groups + span]), axis=0)
        gathered = dot(counts[0], parts)
        for extra in counts[1:]:
            gathered = gathered + dot(extra, parts)
        for i in range(chunk):
            k = first + i
            real = imag = None
            for c in range(types):
                response = response_ref[c, pl.ds(base + k, 1), :]
                response_real, response_imag = response[:, :steps], response[:, steps:]
                start = (i * types + c) * groups
                bucket = gathered[start : start + groups]
                bucket_real, bucket_imag = bucket[:, :steps], bucket[:, steps:]
                term_real = bucket_real * response_real - bucket_imag * response_imag
                term_imag = bucket_real * response_imag + bucket_imag * response_real
                real = term_real if c == 0 else real + term_real
                imag = term_imag if c == 0 else imag + term_imag
            product_ref[pl.ds(k * groups, groups), pl.ds(0, steps)] = real
            product_ref[pl.ds(k * groups, groups), pl.ds(steps, steps)] = imag
    high, low = split(product_ref[...])
    inverse_high = inverse_high_ref[...]
    both = dot(high, jnp.concatenate([inverse_high, inverse_low_ref[...]], axis=1))
    result_ref[...] = both[:, :steps] + both[:, steps:] + dot(low, inverse_high)
    copies = out_ref.shape[0] // (groups * block)
    result = jnp.swapaxes(result_ref[...].reshape(block, groups, steps), 0, 1)
    result = result.reshape(groups * block, steps).astype(BF16)
    for g in range(groups):
        part = result[g * block : (g + 1) * block]
        owner, own = divmod(g, G_DEV)
        for copy in range(copies):
            start = ((copy * readers + owner) * G_DEV + own) * block
            out_ref[pl.ds(start, block), :] = part


def field_kernel(readers, block, column_ref, own_ref, other_ref, incoming_ref, out_ref):
    column = column_ref[:, :1]
    outer = lax.axis_size("outer")
    here = lax.axis_index("outer")
    own = own_ref[...]
    if outer == 1:
        projection = own
    else:
        other = other_ref[...]
        projection = jnp.concatenate(
            [jnp.where(here == x, own, other) for x in range(outer)], axis=1
        )
    field = None
    for g in range(G_DEV):
        incoming = jnp.concatenate(
            [
                incoming_ref[pl.ds(((x * readers + part) * G_DEV + g) * block, block), :]
                for x in range(outer)
                for part in range(readers)
            ],
            axis=0,
        )
        term = dot(projection, incoming)
        field = term if g == 0 else jnp.where(column == g, term, field)
    out_ref[...] = field


def local(
    currents,
    basis_group,
    projection,
    filters,
    pair_src,
    pair_dst,
    pair_type,
    live_count,
    send_group,
    recv_group,
):
    readers = lax.axis_size("grp")
    outer = lax.axis_size("outer")
    inner = lax.axis_size("inner")
    steps = currents.shape[1]
    basis, width = projection.shape
    types, taps, _ = filters.shape
    slots = pair_src.shape[0]
    block = width // readers
    groups = readers * G_DEV
    rows = G_DEV * block + TABLE_ROWS
    (forward_high, forward_low), (inverse_high, inverse_low) = wave_tables(steps)
    group_row = basis_group.reshape(1, basis)

    inputs = (
        currents,
        group_row,
        projection,
        pair_src,
        pair_dst,
        pair_type,
        live_count.reshape(1, 1),
        send_group,
        recv_group,
    )
    outgoing = pl.pallas_call(
        functools.partial(project_kernel, readers, slots),
        out_shape=jax.ShapeDtypeStruct((readers, rows, steps), BF16),
        in_specs=[FAR] * len(inputs),
        out_specs=VMEM,
        scratch_shapes=[pltpu.VMEM(x.shape, x.dtype) for x in inputs[:3]]
        + [pltpu.SMEM(x.shape, x.dtype) for x in inputs[3:]]
        + [pltpu.SemaphoreType.DMA((len(inputs),))],
    )(*inputs)
    arrived = lax.all_to_all(outgoing, "grp", split_axis=0, concat_axis=0, tiled=True)
    partner = lax.ppermute(projection, "outer", [(0, 1), (1, 0)])
    response, column = pl.pallas_call(
        filter_kernel,
        out_shape=(
            pltpu.VMEM((types, width, 2 * steps), F32),
            pltpu.VMEM((basis, LANES), F32),
        ),
        in_specs=[VMEM, VMEM, VMEM],
        out_specs=(VMEM, VMEM),
        compiler_params=PARAMS,
        cost_estimate=pl.CostEstimate(
            flops=8 * types * width * taps * steps, bytes_accessed=2**21, transcendentals=0
        ),
    )(group_row, filters, np.concatenate([forward_high[:taps], forward_low[:taps]], axis=0))
    arrived, partner = lax.optimization_barrier((arrived, partner))
    incoming = pl.pallas_call(
        functools.partial(translate_kernel, readers, slots, block),
        out_shape=pltpu.VMEM((outer * groups * block, steps), BF16),
        in_specs=[VMEM, VMEM, VMEM, VMEM, VMEM],
        out_specs=VMEM,
        compiler_params=PARAMS,
        scratch_shapes=[
            pltpu.VMEM((groups * block, steps), F32),
            pltpu.VMEM((groups * block, steps), BF16),
            pltpu.VMEM((groups * block, 2 * steps), F32),
            pltpu.VMEM((groups * block, steps), F32),
        ],
    )(
        near(arrived.reshape(readers * rows, steps)),
        near(response),
        near(jnp.asarray(np.concatenate([forward_high, forward_low], axis=0))),
        near(jnp.asarray(inverse_high)),
        near(jnp.asarray(inverse_low)),
    )
    incoming = incoming.reshape(outer * readers, G_DEV * block, steps)
    own = lax.all_to_all(incoming, ("outer", "grp"), split_axis=0, concat_axis=0, tiled=True)
    term = pl.pallas_call(
        functools.partial(field_kernel, readers, block),
        out_shape=pltpu.VMEM((basis, steps), F32),
        in_specs=[VMEM, VMEM, VMEM, VMEM],
        out_specs=VMEM,
        compiler_params=PARAMS,
    )(
        near(column),
        near(projection),
        near(partner),
        near(own.reshape(outer * groups * block, steps)),
    )
    total = term
    if inner > 1:
        total = term + lax.ppermute(term, "inner", [(0, 1), (1, 0)])
    return total.astype(BF16)


def solution(mesh):
    readers, spans = mesh.devices.shape
    split_mesh = jax.sharding.Mesh(
        mesh.devices.reshape(readers, spans // 2, 2), ("grp", "outer", "inner")
    )
    return jax.shard_map(
        local,
        mesh=split_mesh,
        in_specs=(
            P("grp", None),
            P("grp"),
            P("grp", ("outer", "inner")),
            P(None, None, ("outer", "inner")),
            P("grp"),
            P("grp"),
            P("grp"),
            P("grp"),
            P(),
            P(),
        ),
        out_specs=P("grp", None),
        check_vma=False,
    )
```

```python
import functools
import math

import jax
import jax.numpy as jnp
import numpy as np
from jax import lax
from jax.experimental import pallas as pl
from jax.experimental.pallas import tpu as pltpu
from jax.sharding import PartitionSpec as P

G_DEV = 2
LANES = 128
TABLE_ROWS = 8
BF16 = jnp.bfloat16
F32 = jnp.float32

VMEM = pl.BlockSpec(memory_space=pltpu.VMEM)
FAR = pl.BlockSpec(memory_space=pl.ANY)
PARAMS = pltpu.CompilerParams(vmem_limit_bytes=16 * 2**20)


def near(value):
    return pltpu.with_memory_space_constraint(value, pltpu.VMEM)


def halves(table):
    high = table.astype(jnp.bfloat16)
    low = (table - high.astype(np.float64)).astype(jnp.bfloat16)
    return high, low


def wave_tables(steps):
    angle = np.pi * np.outer(np.arange(steps), np.arange(steps) + 0.5) / steps
    forward = np.concatenate([np.cos(angle), -np.sin(angle)], axis=1)
    inverse = forward.T / steps
    return halves(forward), halves(inverse)


def dot(a, b, dims=((1,), (0,))):
    return lax.dot_general(a, b, (dims, ((), ())), preferred_element_type=F32)


def project_kernel(
    readers,
    slots,
    currents_hbm,
    group_hbm,
    projection_hbm,
    src_hbm,
    dst_hbm,
    type_hbm,
    live_hbm,
    send_hbm,
    recv_hbm,
    filters_hbm,
    table_hbm,
    out_ref,
    response_ref,
    column_ref,
    currents_ref,
    group_ref,
    projection_ref,
    src_ref,
    dst_ref,
    type_ref,
    live_ref,
    send_ref,
    recv_ref,
    filters_ref,
    table_ref,
    sems,
):
    moves = [
        (filters_hbm, filters_ref),
        (table_hbm, table_ref),
        (group_hbm, group_ref),
        (src_hbm, src_ref),
        (dst_hbm, dst_ref),
        (type_hbm, type_ref),
        (live_hbm, live_ref),
        (send_hbm, send_ref),
        (recv_hbm, recv_ref),
        (projection_hbm, projection_ref),
        (currents_hbm, currents_ref),
    ]
    copies = [
        pltpu.make_async_copy(source, target, sems.at[i])
        for i, (source, target) in enumerate(moves)
    ]
    for copy in copies:
        copy.start()
    for copy in copies[:3]:
        copy.wait()
    for c in range(filters_ref.shape[0]):
        taps_c = filters_ref[c]
        taps_c = jnp.concatenate([taps_c, taps_c], axis=0)
        response_ref[c] = dot(taps_c, table_ref[...], ((0,), (0,)))
    column_ref[...] = jnp.broadcast_to(
        group_ref[...].astype(F32), (LANES, group_ref.shape[1])
    ).T

    block = projection_ref.shape[1] // readers
    rows = out_ref.shape[1]
    me = lax.axis_index("grp")
    pack = max(1, LANES // slots)
    first = lax.rem(me, pack) * slots
    lane = lax.broadcasted_iota(jnp.int32, (TABLE_ROWS, LANES), 1)
    row = lax.broadcasted_iota(jnp.int32, (TABLE_ROWS, LANES), 0)
    for copy in copies[3:]:
        copy.wait()
    live = live_ref[0, 0]

    def add_slot(p, table):
        src = src_ref[p]
        dst = dst_ref[p]
        source = src * G_DEV + send_ref[src, me]
        target = dst * G_DEV + recv_ref[dst, me] + 1
        target = jnp.where(p < live, target, 0)
        value = jnp.where(row == 0, source, jnp.where(row == 1, target, type_ref[p]))
        return jnp.where(lane == first + p, value, table)

    table = lax.fori_loop(
        0, slots, add_slot, jnp.zeros((TABLE_ROWS, LANES), jnp.int32), unroll=slots <= 16
    )
    table = table.astype(F32).astype(BF16)
    for owner in range(readers):
        out_ref[owner, pl.ds(rows - TABLE_ROWS, TABLE_ROWS), :] = table

    pattern = projection_ref[...].T
    series = currents_ref[...]
    for g in range(G_DEV):
        member = (group_ref[...] == g).astype(F32).astype(BF16)
        signature = dot(pattern * member, series).astype(BF16)
        for owner in range(readers):
            out_ref[owner, pl.ds(g * block, block), :] = signature[
                owner * block : (owner + 1) * block
            ]


def split(value):
    high = value.astype(BF16)
    return high, (value - high.astype(F32)).astype(BF16)


def translate_kernel(
    readers,
    slots,
    block,
    arrived_ref,
    response_ref,
    forward_ref,
    inverse_high_ref,
    inverse_low_ref,
    out_ref,
    order_ref,
    wave_ref,
    product_ref,
    result_ref,
):
    types = response_ref.shape[0]
    steps = inverse_high_ref.shape[1]
    groups = readers * G_DEV
    rows = G_DEV * block + TABLE_ROWS
    base = lax.axis_index("grp") * block

    for owner in range(readers):
        part = arrived_ref[pl.ds(owner * rows, G_DEV * block), :]
        order_ref[pl.ds(owner * G_DEV * block, G_DEV * block), :] = part.astype(F32)

    chunk = math.gcd(block, max(1, LANES // groups))
    span = chunk * groups
    pack = max(1, LANES // slots)
    count = jnp.zeros((types * groups, 2 * span), F32)
    bucket_row = lax.broadcasted_iota(jnp.int32, (types * groups, LANES), 0)
    group_row = lax.broadcasted_iota(jnp.int32, (groups, LANES), 0)
    for first in range(0, readers, pack):
        table = jnp.zeros((TABLE_ROWS, LANES), F32)
        for owner in range(first, min(first + pack, readers)):
            start = owner * rows + G_DEV * block
            table = table + arrived_ref[pl.ds(start, TABLE_ROWS), :].astype(F32)
        table = table.astype(jnp.int32)
        source, target, kind = table[0:1], table[1:2], table[2:3]
        bucket = jnp.where(target > 0, kind * groups + target - 1, -1)
        to_bucket = (bucket_row == bucket).astype(F32).astype(BF16)
        from_group = (group_row == source).astype(F32).astype(BF16)
        from_group = jnp.concatenate([from_group] * (2 * chunk), axis=0)
        count = count + dot(to_bucket, from_group, ((1,), (1,)))
    column = lax.broadcasted_iota(jnp.int32, (1, 2 * span), 1)
    column = jnp.where(column >= span, column - span, column)
    counts = []
    for i in range(chunk):
        own = (column >= i * groups) & (column < (i + 1) * groups)
        counts.append(count * own.astype(F32))
    counts = split(jnp.concatenate(counts, axis=0))
    if readers * slots <= 256:
        counts = counts[:1]

    forward = forward_ref[...]
    signals = order_ref[...].reshape(groups, block, steps)
    signals = jnp.swapaxes(signals, 0, 1).reshape(groups * block, steps).astype(BF16)
    waves = dot(jnp.concatenate([signals, signals], axis=1), forward)
    for first in range(0, block, chunk):
        parts = jnp.concatenate(split(waves[first * groups : first * groups + span]), axis=0)
        gathered = dot(counts[0], parts)
        for extra in counts[1:]:
            gathered = gathered + dot(extra, parts)
        for i in range(chunk):
            k = first + i
            real = imag = None
            for c in range(types):
                response = response_ref[c, pl.ds(base + k, 1), :]
                response_real, response_imag = response[:, :steps], response[:, steps:]
                start = (i * types + c) * groups
                bucket = gathered[start : start + groups]
                bucket_real, bucket_imag = bucket[:, :steps], bucket[:, steps:]
                term_real = bucket_real * response_real - bucket_imag * response_imag
                term_imag = bucket_real * response_imag + bucket_imag * response_real
                real = term_real if c == 0 else real + term_real
                imag = term_imag if c == 0 else imag + term_imag
            product_ref[pl.ds(k * groups, groups), pl.ds(0, steps)] = real
            product_ref[pl.ds(k * groups, groups), pl.ds(steps, steps)] = imag
    high, low = split(product_ref[...])
    inverse_high = inverse_high_ref[...]
    both = dot(high, jnp.concatenate([inverse_high, inverse_low_ref[...]], axis=1))
    result_ref[...] = both[:, :steps] + both[:, steps:] + dot(low, inverse_high)
    copies = out_ref.shape[0] // (groups * block)
    result = jnp.swapaxes(result_ref[...].reshape(block, groups, steps), 0, 1)
    result = result.reshape(groups * block, steps).astype(BF16)
    for g in range(groups):
        part = result[g * block : (g + 1) * block]
        owner, own = divmod(g, G_DEV)
        for copy in range(copies):
            start = ((copy * readers + owner) * G_DEV + own) * block
            out_ref[pl.ds(start, block), :] = part


def field_kernel(readers, block, column_ref, own_ref, other_ref, incoming_ref, out_ref):
    column = column_ref[:, :1]
    outer = lax.axis_size("outer")
    here = lax.axis_index("outer")
    own = own_ref[...]
    if outer == 1:
        projection = own
    else:
        other = other_ref[...]
        projection = jnp.concatenate(
            [jnp.where(here == x, own, other) for x in range(outer)], axis=1
        )
    field = None
    for g in range(G_DEV):
        incoming = jnp.concatenate(
            [
                incoming_ref[pl.ds(((x * readers + part) * G_DEV + g) * block, block), :]
                for x in range(outer)
                for part in range(readers)
            ],
            axis=0,
        )
        term = dot(projection, incoming)
        field = term if g == 0 else jnp.where(column == g, term, field)
    out_ref[...] = field


def local(
    currents,
    basis_group,
    projection,
    filters,
    pair_src,
    pair_dst,
    pair_type,
    live_count,
    send_group,
    recv_group,
):
    readers = lax.axis_size("grp")
    outer = lax.axis_size("outer")
    inner = lax.axis_size("inner")
    steps = currents.shape[1]
    basis, width = projection.shape
    types, taps, _ = filters.shape
    slots = pair_src.shape[0]
    block = width // readers
    groups = readers * G_DEV
    rows = G_DEV * block + TABLE_ROWS
    (forward_high, forward_low), (inverse_high, inverse_low) = wave_tables(steps)
    group_row = basis_group.reshape(1, basis)

    inputs = (
        currents,
        group_row,
        projection,
        pair_src,
        pair_dst,
        pair_type,
        live_count.reshape(1, 1),
        send_group,
        recv_group,
        filters,
        jnp.asarray(np.concatenate([forward_high[:taps], forward_low[:taps]], axis=0)),
    )
    near_table = (0, 1, 2, 9, 10)
    partner = lax.ppermute(projection, "outer", [(0, 1), (1, 0)])
    outgoing, response, column = pl.pallas_call(
        functools.partial(project_kernel, readers, slots),
        out_shape=(
            pltpu.VMEM((readers, rows, steps), BF16),
            pltpu.VMEM((types, width, 2 * steps), F32),
            pltpu.VMEM((basis, LANES), F32),
        ),
        in_specs=[FAR] * len(inputs),
        out_specs=(VMEM, VMEM, VMEM),
        compiler_params=PARAMS,
        scratch_shapes=[
            (pltpu.VMEM if i in near_table else pltpu.SMEM)(x.shape, x.dtype)
            for i, x in enumerate(inputs)
        ]
        + [pltpu.SemaphoreType.DMA((len(inputs),))],
    )(
        *[
            x if x.size == 1 else pltpu.with_memory_space_constraint(x, pltpu.HBM)
            for x in inputs
        ]
    )
    arrived = lax.all_to_all(outgoing, "grp", split_axis=0, concat_axis=0, tiled=True)
    incoming = pl.pallas_call(
        functools.partial(translate_kernel, readers, slots, block),
        out_shape=pltpu.VMEM((outer * groups * block, steps), BF16),
        in_specs=[VMEM, VMEM, VMEM, VMEM, VMEM],
        out_specs=VMEM,
        compiler_params=PARAMS,
        scratch_shapes=[
            pltpu.VMEM((groups * block, steps), F32),
            pltpu.VMEM((groups * block, steps), BF16),
            pltpu.VMEM((groups * block, 2 * steps), F32),
            pltpu.VMEM((groups * block, steps), F32),
        ],
    )(
        near(arrived.reshape(readers * rows, steps)),
        near(response),
        near(jnp.asarray(np.concatenate([forward_high, forward_low], axis=0))),
        near(jnp.asarray(inverse_high)),
        near(jnp.asarray(inverse_low)),
    )
    incoming, partner = lax.optimization_barrier((incoming, partner))
    incoming = incoming.reshape(outer * readers, G_DEV * block, steps)
    own = lax.all_to_all(incoming, ("outer", "grp"), split_axis=0, concat_axis=0, tiled=True)
    term = pl.pallas_call(
        functools.partial(field_kernel, readers, block),
        out_shape=pltpu.VMEM((basis, steps), F32),
        in_specs=[VMEM, VMEM, VMEM, VMEM],
        out_specs=VMEM,
        compiler_params=PARAMS,
    )(
        near(column),
        near(projection),
        near(partner),
        near(own.reshape(outer * groups * block, steps)),
    )
    total = term
    if inner > 1:
        total = term + lax.ppermute(term, "inner", [(0, 1), (1, 0)])
    return total.astype(BF16)


def solution(mesh):
    readers, spans = mesh.devices.shape
    split_mesh = jax.sharding.Mesh(
        mesh.devices.reshape(readers, spans // 2, 2), ("grp", "outer", "inner")
    )
    return jax.shard_map(
        local,
        mesh=split_mesh,
        in_specs=(
            P("grp", None),
            P("grp"),
            P("grp", ("outer", "inner")),
            P(None, None, ("outer", "inner")),
            P("grp"),
            P("grp"),
            P("grp"),
            P("grp"),
            P(),
            P(),
        ),
        out_specs=P("grp", None),
        check_vma=False,
    )
```

```python
import functools
import math

import jax
import jax.numpy as jnp
import numpy as np
from jax import lax
from jax.experimental import pallas as pl
from jax.experimental.pallas import tpu as pltpu
from jax.sharding import PartitionSpec as P

G_DEV = 2
LANES = 128
TABLE_ROWS = 8
BF16 = jnp.bfloat16
F32 = jnp.float32

VMEM = pl.BlockSpec(memory_space=pltpu.VMEM)
FAR = pl.BlockSpec(memory_space=pl.ANY)
PARAMS = pltpu.CompilerParams(vmem_limit_bytes=16 * 2**20)


def near(value):
    return pltpu.with_memory_space_constraint(value, pltpu.VMEM)


def halves(table):
    high = table.astype(jnp.bfloat16)
    low = (table - high.astype(np.float64)).astype(jnp.bfloat16)
    return high, low


def wave_tables(steps):
    angle = np.pi * np.outer(np.arange(steps), np.arange(steps) + 0.5) / steps
    forward = np.concatenate([np.cos(angle), -np.sin(angle)], axis=1)
    inverse = forward.T / steps
    return halves(forward), halves(inverse)


def dot(a, b, dims=((1,), (0,))):
    return lax.dot_general(a, b, (dims, ((), ())), preferred_element_type=F32)


def project_kernel(
    readers,
    slots,
    currents_hbm,
    group_hbm,
    projection_hbm,
    src_hbm,
    dst_hbm,
    type_hbm,
    live_hbm,
    send_hbm,
    recv_hbm,
    filters_hbm,
    table_hbm,
    out_ref,
    response_ref,
    column_ref,
    currents_ref,
    group_ref,
    projection_ref,
    src_ref,
    dst_ref,
    type_ref,
    live_ref,
    send_ref,
    recv_ref,
    filters_ref,
    table_ref,
    sems,
):
    width, window = filters_hbm.shape[2], response_ref.shape[1]
    base = lax.axis_index("grp") * (width // readers)
    near = filters_hbm
    if window < width:
        start = pl.multiple_of(lax.div(base, window) * window, LANES)
        near = filters_hbm.at[:, :, pl.ds(start, window)]
    moves = [
        (src_hbm, src_ref),
        (dst_hbm, dst_ref),
        (type_hbm, type_ref),
        (live_hbm, live_ref),
        (send_hbm, send_ref),
        (recv_hbm, recv_ref),
        (group_hbm, group_ref),
        (projection_hbm, projection_ref),
        (currents_hbm, currents_ref),
        (table_hbm, table_ref),
        (near, filters_ref),
    ]
    copies = [
        pltpu.make_async_copy(source, target, sems.at[i])
        for i, (source, target) in enumerate(moves)
    ]
    for copy in copies:
        copy.start()

    block = projection_ref.shape[1] // readers
    rows = out_ref.shape[1]
    me = lax.axis_index("grp")
    pack = max(1, LANES // slots)
    first = lax.rem(me, pack) * slots
    lane = lax.broadcasted_iota(jnp.int32, (TABLE_ROWS, LANES), 1)
    row = lax.broadcasted_iota(jnp.int32, (TABLE_ROWS, LANES), 0)
    for copy in copies[:9]:
        copy.wait()
    live = live_ref[0, 0]

    def add_slot(p, table):
        src = src_ref[p]
        dst = dst_ref[p]
        source = src * G_DEV + send_ref[src, me]
        target = dst * G_DEV + recv_ref[dst, me] + 1
        target = jnp.where(p < live, target, 0)
        value = jnp.where(row == 0, source, jnp.where(row == 1, target, type_ref[p]))
        return jnp.where(lane == first + p, value, table)

    table = lax.fori_loop(
        0, slots, add_slot, jnp.zeros((TABLE_ROWS, LANES), jnp.int32), unroll=slots <= 16
    )
    table = table.astype(F32).astype(BF16)
    for owner in range(readers):
        out_ref[owner, pl.ds(rows - TABLE_ROWS, TABLE_ROWS), :] = table

    pattern = projection_ref[...].T
    series = currents_ref[...]
    for g in range(G_DEV):
        member = (group_ref[...] == g).astype(F32).astype(BF16)
        signature = dot(pattern * member, series).astype(BF16)
        for owner in range(readers):
            out_ref[owner, pl.ds(g * block, block), :] = signature[
                owner * block : (owner + 1) * block
            ]
    column_ref[...] = jnp.broadcast_to(
        group_ref[...].astype(F32), (LANES, group_ref.shape[1])
    ).T
    for copy in copies[9:]:
        copy.wait()
    for c in range(filters_ref.shape[0]):
        taps_c = filters_ref[c]
        taps_c = jnp.concatenate([taps_c, taps_c], axis=0)
        response_ref[c] = dot(taps_c, table_ref[...], ((0,), (0,)))


def split(value):
    high = value.astype(BF16)
    return high, (value - high.astype(F32)).astype(BF16)


def translate_kernel(
    readers,
    slots,
    block,
    arrived_ref,
    response_ref,
    forward_ref,
    inverse_high_ref,
    inverse_low_ref,
    out_ref,
    order_ref,
    wave_ref,
    product_ref,
    result_ref,
):
    types = response_ref.shape[0]
    steps = inverse_high_ref.shape[1]
    groups = readers * G_DEV
    rows = G_DEV * block + TABLE_ROWS
    base = lax.rem(lax.axis_index("grp") * block, response_ref.shape[1])

    for owner in range(readers):
        part = arrived_ref[pl.ds(owner * rows, G_DEV * block), :]
        order_ref[pl.ds(owner * G_DEV * block, G_DEV * block), :] = part.astype(F32)

    chunk = math.gcd(block, max(1, LANES // groups))
    span = chunk * groups
    pack = max(1, LANES // slots)
    count = jnp.zeros((types * groups, 2 * span), F32)
    bucket_row = lax.broadcasted_iota(jnp.int32, (types * groups, LANES), 0)
    group_row = lax.broadcasted_iota(jnp.int32, (groups, LANES), 0)
    for first in range(0, readers, pack):
        table = jnp.zeros((TABLE_ROWS, LANES), F32)
        for owner in range(first, min(first + pack, readers)):
            start = owner * rows + G_DEV * block
            table = table + arrived_ref[pl.ds(start, TABLE_ROWS), :].astype(F32)
        table = table.astype(jnp.int32)
        source, target, kind = table[0:1], table[1:2], table[2:3]
        bucket = jnp.where(target > 0, kind * groups + target - 1, -1)
        to_bucket = (bucket_row == bucket).astype(F32).astype(BF16)
        from_group = (group_row == source).astype(F32).astype(BF16)
        from_group = jnp.concatenate([from_group] * (2 * chunk), axis=0)
        count = count + dot(to_bucket, from_group, ((1,), (1,)))
    column = lax.broadcasted_iota(jnp.int32, (1, 2 * span), 1)
    column = jnp.where(column >= span, column - span, column)
    counts = []
    for i in range(chunk):
        own = (column >= i * groups) & (column < (i + 1) * groups)
        counts.append(count * own.astype(F32))
    counts = split(jnp.concatenate(counts, axis=0))
    if readers * slots <= 256:
        counts = counts[:1]

    forward = forward_ref[...]
    signals = order_ref[...].reshape(groups, block, steps)
    signals = jnp.swapaxes(signals, 0, 1).reshape(groups * block, steps).astype(BF16)
    waves = dot(jnp.concatenate([signals, signals], axis=1), forward)
    for first in range(0, block, chunk):
        parts = jnp.concatenate(split(waves[first * groups : first * groups + span]), axis=0)
        gathered = dot(counts[0], parts)
        for extra in counts[1:]:
            gathered = gathered + dot(extra, parts)
        for i in range(chunk):
            k = first + i
            real = imag = None
            for c in range(types):
                response = response_ref[c, pl.ds(base + k, 1), :]
                response_real, response_imag = response[:, :steps], response[:, steps:]
                start = (i * types + c) * groups
                bucket = gathered[start : start + groups]
                bucket_real, bucket_imag = bucket[:, :steps], bucket[:, steps:]
                term_real = bucket_real * response_real - bucket_imag * response_imag
                term_imag = bucket_real * response_imag + bucket_imag * response_real
                real = term_real if c == 0 else real + term_real
                imag = term_imag if c == 0 else imag + term_imag
            product_ref[pl.ds(k * groups, groups), pl.ds(0, steps)] = real
            product_ref[pl.ds(k * groups, groups), pl.ds(steps, steps)] = imag
    high, low = split(product_ref[...])
    inverse_high = inverse_high_ref[...]
    both = dot(high, jnp.concatenate([inverse_high, inverse_low_ref[...]], axis=1))
    result_ref[...] = both[:, :steps] + both[:, steps:] + dot(low, inverse_high)
    copies = out_ref.shape[0] // (groups * block)
    result = jnp.swapaxes(result_ref[...].reshape(block, groups, steps), 0, 1)
    result = result.reshape(groups * block, steps).astype(BF16)
    for g in range(groups):
        part = result[g * block : (g + 1) * block]
        owner, own = divmod(g, G_DEV)
        for copy in range(copies):
            start = ((copy * readers + owner) * G_DEV + own) * block
            out_ref[pl.ds(start, block), :] = part


def field_kernel(readers, block, column_ref, own_ref, other_ref, incoming_ref, out_ref):
    column = column_ref[:, :1]
    outer = lax.axis_size("outer")
    here = lax.axis_index("outer")
    own = own_ref[...]
    if outer == 1:
        projection = own
    else:
        other = other_ref[...]
        projection = jnp.concatenate(
            [jnp.where(here == x, own, other) for x in range(outer)], axis=1
        )
    field = None
    for g in range(G_DEV):
        incoming = jnp.concatenate(
            [
                incoming_ref[pl.ds(((x * readers + part) * G_DEV + g) * block, block), :]
                for x in range(outer)
                for part in range(readers)
            ],
            axis=0,
        )
        term = dot(projection, incoming)
        field = term if g == 0 else jnp.where(column == g, term, field)
    out_ref[...] = field


def local(
    currents,
    basis_group,
    projection,
    filters,
    pair_src,
    pair_dst,
    pair_type,
    live_count,
    send_group,
    recv_group,
):
    readers = lax.axis_size("grp")
    outer = lax.axis_size("outer")
    inner = lax.axis_size("inner")
    steps = currents.shape[1]
    basis, width = projection.shape
    types, taps, _ = filters.shape
    slots = pair_src.shape[0]
    block = width // readers
    groups = readers * G_DEV
    rows = G_DEV * block + TABLE_ROWS
    (forward_high, forward_low), (inverse_high, inverse_low) = wave_tables(steps)
    group_row = basis_group.reshape(1, basis)

    inputs = (
        currents,
        group_row,
        projection,
        pair_src,
        pair_dst,
        pair_type,
        live_count.reshape(1, 1),
        send_group,
        recv_group,
        filters,
        jnp.asarray(np.concatenate([forward_high[:taps], forward_low[:taps]], axis=0)),
    )
    near_table = (0, 1, 2, 9, 10)
    window = LANES if width % LANES == 0 and LANES % block == 0 else width
    partner = lax.ppermute(projection, "outer", [(0, 1), (1, 0)])
    outgoing, response, column = pl.pallas_call(
        functools.partial(project_kernel, readers, slots),
        out_shape=(
            pltpu.VMEM((readers, rows, steps), BF16),
            pltpu.VMEM((types, window, 2 * steps), F32),
            pltpu.VMEM((basis, LANES), F32),
        ),
        in_specs=[FAR] * len(inputs),
        out_specs=(VMEM, VMEM, VMEM),
        compiler_params=PARAMS,
        scratch_shapes=[
            (pltpu.VMEM if i in near_table else pltpu.SMEM)(
                (types, taps, window) if x is filters else x.shape, x.dtype
            )
            for i, x in enumerate(inputs)
        ]
        + [pltpu.SemaphoreType.DMA((len(inputs),))],
    )(
        *[
            x if x.size == 1 else pltpu.with_memory_space_constraint(x, pltpu.HBM)
            for x in inputs
        ]
    )
    arrived = lax.all_to_all(outgoing, "grp", split_axis=0, concat_axis=0, tiled=True)
    incoming = pl.pallas_call(
        functools.partial(translate_kernel, readers, slots, block),
        out_shape=pltpu.VMEM((outer * groups * block, steps), BF16),
        in_specs=[VMEM, VMEM, VMEM, VMEM, VMEM],
        out_specs=VMEM,
        compiler_params=PARAMS,
        scratch_shapes=[
            pltpu.VMEM((groups * block, steps), F32),
            pltpu.VMEM((groups * block, steps), BF16),
            pltpu.VMEM((groups * block, 2 * steps), F32),
            pltpu.VMEM((groups * block, steps), F32),
        ],
    )(
        near(arrived.reshape(readers * rows, steps)),
        near(response),
        near(jnp.asarray(np.concatenate([forward_high, forward_low], axis=0))),
        near(jnp.asarray(inverse_high)),
        near(jnp.asarray(inverse_low)),
    )
    incoming, partner = lax.optimization_barrier((incoming, partner))
    incoming = incoming.reshape(outer * readers, G_DEV * block, steps)
    own = lax.all_to_all(incoming, ("outer", "grp"), split_axis=0, concat_axis=0, tiled=True)
    term = pl.pallas_call(
        functools.partial(field_kernel, readers, block),
        out_shape=pltpu.VMEM((basis, steps), F32),
        in_specs=[VMEM, VMEM, VMEM, VMEM],
        out_specs=VMEM,
        compiler_params=PARAMS,
    )(
        near(column),
        near(projection),
        near(partner),
        near(own.reshape(outer * groups * block, steps)),
    )
    total = term
    if inner > 1:
        total = term + lax.ppermute(term, "inner", [(0, 1), (1, 0)])
    return total.astype(BF16)


def solution(mesh):
    readers, spans = mesh.devices.shape
    split_mesh = jax.sharding.Mesh(
        mesh.devices.reshape(readers, spans // 2, 2), ("grp", "outer", "inner")
    )
    return jax.shard_map(
        local,
        mesh=split_mesh,
        in_specs=(
            P("grp", None),
            P("grp"),
            P("grp", ("outer", "inner")),
            P(None, None, ("outer", "inner")),
            P("grp"),
            P("grp"),
            P("grp"),
            P("grp"),
            P(),
            P(),
        ),
        out_specs=P("grp", None),
        check_vma=False,
    )
```
